32 devices in a mesh: dp: 8 (over y, x, core), tensor: 4 (over z).
Axes of the slice: x: 2, y: 2, z: 4, core: 2. Of those that a mesh axis runs over, the one named last changes fastest.
Arguments:
- tokens_in: bfloat16 [4096, 1024], P(('dp', 'tensor')), may hold values from -6 to 6
- attn_gain: float32 [1024], replicated, may hold values from 0.1 to 1.9
- w_query: bfloat16 [1024, 2048], P(None, 'tensor'), may hold values from -0.1875 to 0.1875
- w_key: bfloat16 [1024, 1024], P(None, 'tensor'), may hold values from -0.1875 to 0.1875
- w_value: bfloat16 [1024, 1024], P(None, 'tensor'), may hold values from -0.1875 to 0.1875
- query_gain: float32 [128], replicated, may hold values from 0.5 to 2.5, as said below
- key_gain: float32 [128], replicated, may hold values from 0.5 to 2.5, as said below
- w_output: bfloat16 [2048, 1024], P('tensor'), may hold values from -0.5 to 0.5
- mlp_gain: float32 [1024], replicated, may hold values from 0.1 to 1.9
- w_gate: bfloat16 [1024, 3072], P(None, 'tensor'), may hold values from -0.1875 to 0.1875
- w_up: bfloat16 [1024, 3072], P(None, 'tensor'), may hold values from -0.1875 to 0.1875
- w_down: bfloat16 [3072, 1024], P('tensor'), may hold values from -0.109375 to 0.109375
- out_cotangent: bfloat16 [4096, 1024], P(('dp', 'tensor')), may hold values from -6 to 6
Outputs:
- block_out: bfloat16 [4096, 1024], P(('dp', 'tensor'))
- grad_input: bfloat16 [4096, 1024], P(('dp', 'tensor'))
- grad_attn_gain: float32 [1024], replicated
- grad_w_query: float32 [1024, 2048], P('dp', 'tensor')
- grad_w_key: float32 [1024, 1024], P('dp', 'tensor')
- grad_w_value: float32 [1024, 1024], P('dp', 'tensor')
- grad_query_gain: float32 [128], replicated
- grad_key_gain: float32 [128], replicated
- grad_w_output: float32 [2048, 1024], P('tensor', 'dp')
- grad_mlp_gain: float32 [1024], replicated
- grad_w_gate: float32 [1024, 3072], P('dp', 'tensor')
- grad_w_up: float32 [1024, 3072], P('dp', 'tensor')
- grad_w_down: float32 [3072, 1024], P('tensor', 'dp')
The draws below stay inside these ranges and needn't reach their ends.
Inputs may be any that keep to these rules, and one draw needn't show every extreme that they name: `query_gain`: positive gains. `key_gain`: positive gains.
All inputs are finite; a program needn't handle non-finite values.
Results may differ from the reference program's by a relative error of at most 0.025.
Values may be sent and summed in bfloat16 or wider, within the bound.
A program may use at most 128 MiB of HBM per device.

```python
import math
import jax
import jax.numpy as jnp
from jax import lax

D = 1024
HEADS = 16
KV_HEADS = 8
HEAD_DIM = 128
FF = 3072
SEQ = 512
TOKENS = 4096
N_TENSOR = 4


def gain_values(key):
    return jnp.exp(jax.random.uniform(key, (HEAD_DIM,), jnp.float32, math.log(0.5), math.log(2.5)))


def draw_query_gain(key, part):
    return gain_values(jax.random.fold_in(key, 11))


def draw_key_gain(key, part):
    return gain_values(jax.random.fold_in(key, 23))


def raised(result, own_key, source, target, shards_of, factor):
    def block_of(position):
        return (jnp.arange(result.shape[position]) // (result.shape[position] // shards_of)).reshape((-1,) + (1,) * (result.ndim - 1 - position))

    near = jax.random.permutation(own_key, shards_of)[block_of(target)]
    second = (block_of(target) + shards_of // 2) % shards_of
    return jnp.where((block_of(source) == near) | (block_of(source) == second), factor * result, result)


def shard_levels(own_key, shape, pieces, least, largest):
    def one(axis_at, shards_of):
        heights = jax.random.uniform(jax.random.fold_in(jax.random.fold_in(own_key, 6), axis_at), (shards_of,), jnp.float32, least / len(pieces), largest / len(pieces))
        return jnp.repeat(jnp.exp(heights), shape[axis_at] // shards_of).reshape((-1,) + (1,) * (len(shape) - axis_at - 1))

    factor_of = one(*pieces[0])
    for cut in pieces[1:]:
        factor_of = factor_of * one(*cut)
    return factor_of


def normal_values(own_key, dims, spread, limit, split=(), held_as=jnp.bfloat16):
    gain = shard_levels(own_key, dims, split, -0.22, 0.18) if split else 1.0
    drawn = jax.random.normal(own_key, dims, jnp.float32) * spread * gain
    return jnp.minimum(jnp.maximum(drawn, -limit), limit).astype(held_as)


def gaussian_with(stream_key, shape, width, limit, split, heavy, kind=jnp.bfloat16):
    values = width * jax.random.normal(stream_key, shape, jnp.float32)
    if split:
        values = values * shard_levels(stream_key, shape, split, -0.22, 0.18)
    return jnp.clip(raised(values, jax.random.fold_in(stream_key, 3), *heavy), -limit, limit).astype(kind)


def setup_inputs(seed: int = 0) -> dict:
    splits = jax.random.split(jax.random.key(seed), 14)
    tokens_in = gaussian_with(splits[0], (TOKENS, D), 1.0, 6.0, ((0, 32),), (0, 1, 32, 2.75))
    attn_gain = jnp.clip(1.0 + 0.18 * jax.random.normal(splits[1], (D,), jnp.float32), 0.1, 1.9)
    w_query = normal_values(splits[2], (D, HEADS * HEAD_DIM), D ** -0.5, 0.1875, ((1, 4),))
    w_key = normal_values(splits[3], (D, KV_HEADS * HEAD_DIM), D ** -0.5, 0.1875, ((1, 4),))
    w_value = normal_values(splits[4], (D, KV_HEADS * HEAD_DIM), D ** -0.5, 0.1875, ((1, 4),))
    query_gain = draw_query_gain(jax.random.fold_in(splits[13], 71), 0)
    key_gain = draw_key_gain(jax.random.fold_in(splits[13], 71), 0)
    w_output = normal_values(splits[7], (HEADS * HEAD_DIM, D), (HEADS * HEAD_DIM // 16) ** -0.5, 0.5, ((0, 4),))
    mlp_gain = jnp.clip(1.0 + 0.18 * jax.random.normal(splits[8], (D,), jnp.float32), 0.1, 1.9)
    w_gate = normal_values(splits[9], (D, FF), D ** -0.5, 0.1875, ((1, 4),))
    w_up = normal_values(splits[10], (D, FF), D ** -0.5, 0.1875, ((1, 4),))
    w_down = normal_values(splits[11], (FF, D), FF ** -0.5, 0.109375, ((0, 4),))
    out_cotangent = gaussian_with(splits[12], (TOKENS, D), 1.0, 6.0, ((0, 32),), (0, 1, 32, 2.75))
    return dict(tokens_in=tokens_in, attn_gain=attn_gain, w_query=w_query, w_key=w_key, w_value=w_value, query_gain=query_gain, key_gain=key_gain, w_output=w_output, mlp_gain=mlp_gain, w_gate=w_gate, w_up=w_up, w_down=w_down, out_cotangent=out_cotangent)


EPS = 1e-06
THETA = 1000000.0

def rope_tables(length, head_width):
    half_width = head_width // 2
    inverse_freq = THETA ** (-(jnp.arange(half_width, dtype=jnp.float32) * 2.0 / head_width))
    positions = jnp.arange(length, dtype=jnp.float32)
    angles = positions[:, None] * inverse_freq[None, :]
    return (jnp.cos(angles)[:, None, :], jnp.sin(angles)[:, None, :])

def rope_apply(values, cosine_table, sine_table):
    half_width = values.shape[-1] // 2
    first_half = values[..., :half_width]
    second_half = values[..., half_width:]
    return jnp.concatenate([first_half * cosine_table - second_half * sine_table, second_half * cosine_table + first_half * sine_table], axis=-1)

def rope_back(grad_rows, cosine_table, sine_table):
    half_width = grad_rows.shape[-1] // 2
    first_half = grad_rows[..., :half_width]
    second_half = grad_rows[..., half_width:]
    return jnp.concatenate([first_half * cosine_table + second_half * sine_table, second_half * cosine_table - first_half * sine_table], axis=-1)

def row_scale(values):
    return lax.rsqrt(lax.optimization_barrier(jnp.mean(values * values, axis=-1, keepdims=True)) + EPS)

def norm_back(grad_out, values, scale_rows, gain_row):
    weighted = grad_out * gain_row
    inner_mean = lax.optimization_barrier(jnp.mean(weighted * values, axis=-1, keepdims=True))
    return scale_rows * weighted - values * scale_rows ** 3 * inner_mean

def tensor_partials(left, right):
    groups_left = left.reshape(left.shape[0], N_TENSOR, left.shape[1] // N_TENSOR).astype(jnp.float32)
    groups_right = right.reshape(N_TENSOR, right.shape[0] // N_TENSOR, right.shape[1]).astype(jnp.float32)
    partial_value = jnp.einsum('sgc,gcd->gsd', groups_left, groups_right)
    rounded = lax.optimization_barrier(partial_value.astype(jnp.bfloat16))
    return lax.optimization_barrier(jnp.sum(rounded.astype(jnp.float32), axis=0))

def sequence_pass(x_seq, grad_seq, weights):
    attn_gain, w_query, w_key, w_value, query_gain, key_gain, w_output, mlp_gain, w_gate, w_up, w_down = weights
    ratio = HEADS // KV_HEADS
    factor = HEAD_DIM ** (-0.5)
    cosine_table, sine_table = rope_tables(SEQ, HEAD_DIM)
    resid_in = x_seq.astype(jnp.float32)
    scale_one = row_scale(resid_in)
    normed_one = (resid_in * scale_one * attn_gain).astype(jnp.bfloat16)
    query_lin = jnp.dot(normed_one, w_query, preferred_element_type=jnp.float32).reshape(SEQ, HEADS, HEAD_DIM)
    key_lin = jnp.dot(normed_one, w_key, preferred_element_type=jnp.float32).reshape(SEQ, KV_HEADS, HEAD_DIM)
    value_heads = jnp.dot(normed_one, w_value, preferred_element_type=jnp.float32).astype(jnp.bfloat16).reshape(SEQ, KV_HEADS, HEAD_DIM)
    query_scale = row_scale(query_lin)
    key_scale = row_scale(key_lin)
    query_rot = rope_apply(query_lin * query_scale * query_gain, cosine_table, sine_table).astype(jnp.bfloat16)
    key_rot = rope_apply(key_lin * key_scale * key_gain, cosine_table, sine_table).astype(jnp.bfloat16)
    keys_all = jnp.repeat(key_rot, ratio, axis=1).astype(jnp.float32)
    values_all = jnp.repeat(value_heads, ratio, axis=1).astype(jnp.float32)
    query_float = query_rot.astype(jnp.float32)
    scores = jnp.einsum('qhd,khd->hqk', query_float, keys_all) * factor
    allowed = jnp.arange(SEQ)[None, :] <= jnp.arange(SEQ)[:, None]
    scores = jnp.where(allowed[None, :, :], scores, -jnp.inf)
    top_score = lax.optimization_barrier(jnp.max(scores, axis=-1, keepdims=True))
    log_total = top_score + jnp.log(lax.optimization_barrier(jnp.sum(jnp.exp(scores - top_score), axis=-1, keepdims=True)))
    probs_full = jnp.exp(scores - log_total)
    probs_low = probs_full.astype(jnp.bfloat16)
    mixed_heads = jnp.einsum('hqk,khd->qhd', probs_low.astype(jnp.float32), values_all).astype(jnp.bfloat16)
    attn_flat = mixed_heads.reshape(SEQ, HEADS * HEAD_DIM)
    hidden = resid_in + tensor_partials(attn_flat, w_output)
    scale_two = row_scale(hidden)
    normed_two = (hidden * scale_two * mlp_gain).astype(jnp.bfloat16)
    gate_lin = jnp.dot(normed_two, w_gate, preferred_element_type=jnp.float32)
    up_lin = jnp.dot(normed_two, w_up, preferred_element_type=jnp.float32)
    gate_sig = jax.nn.sigmoid(gate_lin)
    activated = (gate_lin * gate_sig * up_lin).astype(jnp.bfloat16)
    block_out = (hidden + tensor_partials(activated, w_down)).astype(jnp.bfloat16)
    grad_down = jnp.dot(activated.T, grad_seq, preferred_element_type=jnp.float32)
    grad_act = jnp.dot(grad_seq, w_down.T, preferred_element_type=jnp.float32)
    grad_gate = (grad_act * up_lin * gate_sig * (1.0 + gate_lin * (1.0 - gate_sig))).astype(jnp.bfloat16)
    grad_up = (grad_act * gate_lin * gate_sig).astype(jnp.bfloat16)
    grad_w_gate = jnp.dot(normed_two.T, grad_gate, preferred_element_type=jnp.float32)
    grad_w_up = jnp.dot(normed_two.T, grad_up, preferred_element_type=jnp.float32)
    grad_norm_two = jnp.dot(grad_gate, w_gate.T, preferred_element_type=jnp.float32) + jnp.dot(grad_up, w_up.T, preferred_element_type=jnp.float32)
    gain_two = lax.optimization_barrier(jnp.sum(grad_norm_two * hidden * scale_two, axis=0))
    grad_hidden = grad_seq.astype(jnp.float32) + norm_back(grad_norm_two, hidden, scale_two, mlp_gain)
    grad_hidden_low = grad_hidden.astype(jnp.bfloat16)
    grad_w_output = jnp.dot(attn_flat.T, grad_hidden_low, preferred_element_type=jnp.float32)
    grad_mixed = jnp.dot(grad_hidden_low, w_output.T, preferred_element_type=jnp.float32).astype(jnp.bfloat16).reshape(SEQ, HEADS, HEAD_DIM)
    grad_mixed_float = grad_mixed.astype(jnp.float32)
    inner_rows = lax.optimization_barrier(jnp.sum(grad_mixed_float * mixed_heads.astype(jnp.float32), axis=-1)).T[:, :, None]
    grad_probs = jnp.einsum('qhd,khd->hqk', grad_mixed_float, values_all)
    grad_scores = (probs_full * (grad_probs - inner_rows)).astype(jnp.bfloat16).astype(jnp.float32)
    grad_query_rot = jnp.einsum('hqk,khd->qhd', grad_scores, keys_all) * factor
    grad_key_all = jnp.einsum('hqk,qhd->khd', grad_scores, query_float) * factor
    grad_key_rot = lax.optimization_barrier(jnp.sum(grad_key_all.reshape(SEQ, KV_HEADS, ratio, HEAD_DIM), axis=2))
    grad_value_all = jnp.einsum('hqk,qhd->khd', probs_low.astype(jnp.float32), grad_mixed_float)
    grad_values = lax.optimization_barrier(jnp.sum(grad_value_all.reshape(SEQ, KV_HEADS, ratio, HEAD_DIM), axis=2))
    grad_query_pre = rope_back(grad_query_rot, cosine_table, sine_table)
    grad_key_pre = rope_back(grad_key_rot, cosine_table, sine_table)
    gain_query = lax.optimization_barrier(jnp.sum(grad_query_pre * query_lin * query_scale, axis=(0, 1)))
    gain_key = lax.optimization_barrier(jnp.sum(grad_key_pre * key_lin * key_scale, axis=(0, 1)))
    grad_query_low = norm_back(grad_query_pre, query_lin, query_scale, query_gain).astype(jnp.bfloat16).reshape(SEQ, HEADS * HEAD_DIM)
    grad_key_low = norm_back(grad_key_pre, key_lin, key_scale, key_gain).astype(jnp.bfloat16).reshape(SEQ, KV_HEADS * HEAD_DIM)
    grad_value_low = grad_values.astype(jnp.bfloat16).reshape(SEQ, KV_HEADS * HEAD_DIM)
    grad_w_query = jnp.dot(normed_one.T, grad_query_low, preferred_element_type=jnp.float32)
    grad_w_key = jnp.dot(normed_one.T, grad_key_low, preferred_element_type=jnp.float32)
    grad_w_value = jnp.dot(normed_one.T, grad_value_low, preferred_element_type=jnp.float32)
    grad_norm_one = jnp.dot(grad_query_low, w_query.T, preferred_element_type=jnp.float32) + jnp.dot(grad_key_low, w_key.T, preferred_element_type=jnp.float32) + jnp.dot(grad_value_low, w_value.T, preferred_element_type=jnp.float32)
    gain_one = lax.optimization_barrier(jnp.sum(grad_norm_one * resid_in * scale_one, axis=0))
    grad_input = (grad_hidden + norm_back(grad_norm_one, resid_in, scale_one, attn_gain)).astype(jnp.bfloat16)
    grad_terms = (gain_one, grad_w_query, grad_w_key, grad_w_value, gain_query, gain_key, grad_w_output, gain_two, grad_w_gate, grad_w_up, grad_down)
    return (block_out, grad_input, grad_terms)

def reference(tokens_in, attn_gain, w_query, w_key, w_value, query_gain, key_gain, w_output, mlp_gain, w_gate, w_up, w_down, out_cotangent):
    seq_total = tokens_in.shape[0] // SEQ
    inputs_seq = tokens_in.reshape(seq_total, SEQ, D)
    cotangent_seq = out_cotangent.reshape(seq_total, SEQ, D)
    weights = (attn_gain, w_query, w_key, w_value, query_gain, key_gain, w_output, mlp_gain, w_gate, w_up, w_down)
    start_sums = tuple((jnp.zeros(weight.shape, jnp.float32) for weight in weights))

    def advance(carry, pair):
        block_out, grad_input, grad_terms = sequence_pass(pair[0], pair[1], weights)
        return (jax.tree.map(lambda total, term: total + term, carry, grad_terms), (block_out, grad_input))
    totals, outputs = lax.scan(advance, start_sums, (inputs_seq, cotangent_seq))
    block_out = outputs[0].reshape(tokens_in.shape[0], D)
    grad_input = outputs[1].reshape(tokens_in.shape[0], D)
    return (block_out, grad_input, totals[0], totals[1], totals[2], totals[3], totals[4], totals[5], totals[6], totals[7], totals[8], totals[9], totals[10])
```

```python
import jax
import jax.numpy as jnp
from jax import lax
from jax.sharding import PartitionSpec as P


SEQ = 512

EPS = 1e-06
THETA = 1000000.0


def rope_tables(length, head_width):
    half_width = head_width // 2
    inverse_freq = THETA ** (-(jnp.arange(half_width, dtype=jnp.float32) * 2.0 / head_width))
    positions = jnp.arange(length, dtype=jnp.float32)
    angles = positions[:, None] * inverse_freq[None, :]
    return (jnp.cos(angles)[:, None, :], jnp.sin(angles)[:, None, :])


def rope_apply(values, cosine_table, sine_table):
    half_width = values.shape[-1] // 2
    first_half = values[..., :half_width]
    second_half = values[..., half_width:]
    return jnp.concatenate(
        [
            first_half * cosine_table - second_half * sine_table,
            second_half * cosine_table + first_half * sine_table,
        ],
        axis=-1,
    )


def rope_back(grad_rows, cosine_table, sine_table):
    half_width = grad_rows.shape[-1] // 2
    first_half = grad_rows[..., :half_width]
    second_half = grad_rows[..., half_width:]
    return jnp.concatenate(
        [
            first_half * cosine_table + second_half * sine_table,
            second_half * cosine_table - first_half * sine_table,
        ],
        axis=-1,
    )


def row_scale(values):
    return lax.rsqrt(jnp.mean(values * values, axis=-1, keepdims=True) + EPS)


def norm_back(grad_out, values, scale_rows, gain_row):
    weighted = grad_out * gain_row
    inner_mean = jnp.mean(weighted * values, axis=-1, keepdims=True)
    return scale_rows * weighted - values * scale_rows**3 * inner_mean


def causal_scores(grouped, key_seq, factor):
    length = grouped.shape[0]
    scores = (
        jnp.einsum("qgrd,kgd->grqk", grouped, key_seq, preferred_element_type=jnp.float32) * factor
    )
    rows_at = lax.broadcasted_iota(jnp.int32, (length, length), 0)
    cols_at = lax.broadcasted_iota(jnp.int32, (length, length), 1)
    return jnp.where(cols_at <= rows_at, scores, -jnp.inf)


def attend_forward(inputs):
    query_seq, key_seq, value_seq = inputs
    length, head_count, head_width = query_seq.shape
    kv_count = key_seq.shape[1]
    grouped = query_seq.reshape(length, kv_count, head_count // kv_count, head_width)
    scores = causal_scores(grouped, key_seq, head_width ** (-0.5))
    top_score = jnp.max(scores, axis=-1, keepdims=True)
    log_total = top_score + jnp.log(jnp.sum(jnp.exp(scores - top_score), axis=-1, keepdims=True))
    prob_low = jnp.exp(scores - log_total).astype(jnp.bfloat16)
    mixed_seq = jnp.einsum(
        "grqk,kgd->qgrd", prob_low, value_seq, preferred_element_type=jnp.float32
    )
    return (mixed_seq.astype(jnp.bfloat16).reshape(length, head_count, head_width), log_total)


def attend_backward(inputs):
    query_seq, key_seq, value_seq, mixed_seq, log_total, grad_mixed = inputs
    length, head_count, head_width = query_seq.shape
    kv_count = key_seq.shape[1]
    ratio = head_count // kv_count
    factor = head_width ** (-0.5)
    grouped = query_seq.reshape(length, kv_count, ratio, head_width)
    scores = causal_scores(grouped, key_seq, factor)
    prob_full = jnp.exp(scores - log_total)
    prob_low = prob_full.astype(jnp.bfloat16)
    grad_grouped = grad_mixed.reshape(length, kv_count, ratio, head_width)
    inner_rows = jnp.sum(grad_mixed.astype(jnp.float32) * mixed_seq.astype(jnp.float32), axis=-1)
    inner_rows = jnp.transpose(inner_rows.reshape(length, kv_count, ratio), (1, 2, 0))[..., None]
    grad_probs = jnp.einsum(
        "qgrd,kgd->grqk", grad_grouped, value_seq, preferred_element_type=jnp.float32
    )
    grad_scores = (prob_full * (grad_probs - inner_rows)).astype(jnp.bfloat16)
    grad_query = (
        jnp.einsum("grqk,kgd->qgrd", grad_scores, key_seq, preferred_element_type=jnp.float32)
        * factor
    )
    grad_key = (
        jnp.einsum("grqk,qgrd->kgd", grad_scores, grouped, preferred_element_type=jnp.float32)
        * factor
    )
    grad_value = jnp.einsum(
        "grqk,qgrd->kgd", prob_low, grad_grouped, preferred_element_type=jnp.float32
    )
    return (grad_query.reshape(length, head_count, head_width), grad_key, grad_value)


def axis_bits(axis):
    return lax.axis_size(axis).bit_length() - 1


def swap(values, axis, bit):
    count = lax.axis_size(axis)
    return lax.ppermute(values, axis, [(i, i ^ (1 << bit)) for i in range(count)])


def rotate(values, axis, step):
    count = lax.axis_size(axis)
    return lax.ppermute(values, axis, [(i, (i + step) % count) for i in range(count)])


def gather_rows(values, axis):
    count = lax.axis_size(axis)
    me = lax.axis_index(axis)
    rows = values.shape[0]
    parts = [values] + [rotate(values, axis, step) for step in range(1, count)]
    full = jnp.zeros((count * rows,) + values.shape[1:], values.dtype)
    for step, part in enumerate(parts):
        owner = lax.rem(me - step + count, count)
        full = lax.dynamic_update_slice_in_dim(full, part, owner * rows, 0)
    return full


def scatter_rows(values, axis):
    count = lax.axis_size(axis)
    me = lax.axis_index(axis)
    rows = values.shape[0] // count

    def block(owner):
        return lax.dynamic_slice_in_dim(values, owner * rows, rows, 0)

    got = [
        rotate(block(lax.rem(me + step, count)), axis, step) for step in range(1, count)
    ]
    total = block(me).astype(jnp.float32)
    for part in got:
        total = total + part.astype(jnp.float32)
    return total


def total_sum(values, axes):
    for axis in axes:
        for bit in range(axis_bits(axis)):
            values = values + swap(values, axis, bit)
    return values


def pick_columns(values, axis, which):
    count = lax.axis_size(axis)
    width = values.shape[1] // count
    return jnp.concatenate(
        [
            lax.dynamic_slice_in_dim(values, (2 * j + which) * width, width, 1)
            for j in range(count // 2)
        ],
        axis=1,
    )


def split_columns(values, axis):
    low = lax.rem(lax.axis_index(axis), 2)
    return pick_columns(values, axis, 1 - low), pick_columns(values, axis, low)


def outer(left, right):
    return lax.dot_general(
        left, right, (((0,), (0,)), ((), ())), preferred_element_type=jnp.float32
    ).astype(jnp.bfloat16)


def weight_grad(split, right, axis, rising):
    away, home = split
    bits = axis_bits(axis)
    me = lax.axis_index(axis)
    shape = (2,) * (bits - 1)
    got = swap(outer(away, right), axis, 0)
    keep = outer(home, right)
    tail = (keep.shape[0] >> (bits - 1), keep.shape[1])
    keep = keep.reshape(shape + tail)
    got = got.reshape(shape + tail)
    left_bits = list(range(bits - 1, 0, -1))
    todo = list(range(1, bits))
    for bit in todo if rising else todo[::-1]:
        at = left_bits.index(bit)
        mine = lax.rem(lax.shift_right_logical(me, bit), 2)

        def half(which):
            part = lax.dynamic_index_in_dim(keep, which, at, False).astype(jnp.float32)
            other = lax.dynamic_index_in_dim(got, which, at, False).astype(jnp.float32)
            return (part + other).astype(jnp.bfloat16)

        sent, keep = half(1 - mine), half(mine)
        got = swap(sent, axis, bit)
        left_bits.remove(bit)
    return keep.astype(jnp.float32) + got.astype(jnp.float32)


def on_device(
    tokens_in,
    attn_gain,
    w_query,
    w_key,
    w_value,
    query_gain,
    key_gain,
    w_output,
    mlp_gain,
    w_gate,
    w_up,
    w_down,
    out_cotangent,
):
    f32 = jnp.float32
    head_width = query_gain.shape[0]
    head_count = w_query.shape[1] // head_width
    kv_count = w_key.shape[1] // head_width
    cosine_table, sine_table = rope_tables(SEQ, head_width)
    resid = tokens_in.astype(f32)
    scale_one = row_scale(resid)
    normed_own = (resid * scale_one * attn_gain).astype(jnp.bfloat16)
    normed_one = gather_rows(normed_own, "tensor")
    normed_one, cotangent = lax.optimization_barrier((normed_one, out_cotangent))
    grad_all = gather_rows(cotangent, "tensor")
    tok_count = normed_one.shape[0]
    seq_count = tok_count // SEQ
    query_lin = jnp.dot(normed_one, w_query, preferred_element_type=f32).reshape(
        tok_count, head_count, head_width
    )
    key_lin = jnp.dot(normed_one, w_key, preferred_element_type=f32).reshape(
        tok_count, kv_count, head_width
    )
    value_heads = (
        jnp.dot(normed_one, w_value, preferred_element_type=f32)
        .astype(jnp.bfloat16)
        .reshape(seq_count, SEQ, kv_count, head_width)
    )
    query_scale = row_scale(query_lin)
    key_scale = row_scale(key_lin)
    query_rot = rope_apply(
        (query_lin * query_scale * query_gain).reshape(seq_count, SEQ, head_count, head_width),
        cosine_table,
        sine_table,
    ).astype(jnp.bfloat16)
    key_rot = rope_apply(
        (key_lin * key_scale * key_gain).reshape(seq_count, SEQ, kv_count, head_width),
        cosine_table,
        sine_table,
    ).astype(jnp.bfloat16)
    mixed_heads, log_totals = lax.map(attend_forward, (query_rot, key_rot, value_heads))
    attn_flat = mixed_heads.reshape(tok_count, head_count * head_width)
    attn_part = jnp.dot(attn_flat, w_output, preferred_element_type=f32).astype(jnp.bfloat16)
    hidden = resid + scatter_rows(attn_part, "tensor")
    scale_two = row_scale(hidden)
    normed_two = gather_rows(
        (hidden * scale_two * mlp_gain).astype(jnp.bfloat16), "tensor"
    )
    gate_lin = jnp.dot(normed_two, w_gate, preferred_element_type=f32)
    up_lin = jnp.dot(normed_two, w_up, preferred_element_type=f32)
    gate_sig = jax.nn.sigmoid(gate_lin)
    activated = (gate_lin * gate_sig * up_lin).astype(jnp.bfloat16)
    grad_act = jnp.dot(grad_all, w_down.T, preferred_element_type=f32)
    grad_gate = (grad_act * up_lin * gate_sig * (1.0 + gate_lin * (1.0 - gate_sig))).astype(
        jnp.bfloat16
    )
    grad_up = (grad_act * gate_lin * gate_sig).astype(jnp.bfloat16)
    back_two = (
        jnp.dot(grad_gate, w_gate.T, preferred_element_type=f32)
        + jnp.dot(grad_up, w_up.T, preferred_element_type=f32)
    ).astype(jnp.bfloat16)
    grad_norm_two = scatter_rows(back_two, "tensor")
    grad_hidden = out_cotangent.astype(f32) + norm_back(
        grad_norm_two, hidden, scale_two, mlp_gain
    )
    gain_two = jnp.sum(grad_norm_two * hidden * scale_two, axis=0)
    grad_hidden_low = gather_rows(grad_hidden.astype(jnp.bfloat16), "tensor")
    activated_late, _ = lax.optimization_barrier((activated, grad_norm_two))
    mlp_part = jnp.dot(activated_late, w_down, preferred_element_type=f32).astype(jnp.bfloat16)
    block_out = (hidden + scatter_rows(mlp_part, "tensor")).astype(jnp.bfloat16)
    split_two = split_columns(normed_two, "dp")
    grad_w_gate = weight_grad(split_two, grad_gate, "dp", True)
    grad_w_up = weight_grad(split_two, grad_up, "dp", False)
    grad_down = weight_grad(split_columns(grad_all, "dp"), activated, "dp", True).T
    grad_w_output = weight_grad(split_columns(grad_hidden_low, "dp"), attn_flat, "dp", False).T
    grad_mixed = (
        jnp.dot(grad_hidden_low, w_output.T, preferred_element_type=f32)
        .astype(jnp.bfloat16)
        .reshape(seq_count, SEQ, head_count, head_width)
    )
    grad_query_rot, grad_key_rot, grad_values = lax.map(
        attend_backward, (query_rot, key_rot, value_heads, mixed_heads, log_totals, grad_mixed)
    )
    grad_query_pre = rope_back(grad_query_rot, cosine_table, sine_table).reshape(
        tok_count, head_count, head_width
    )
    grad_key_pre = rope_back(grad_key_rot, cosine_table, sine_table).reshape(
        tok_count, kv_count, head_width
    )
    gain_query = jnp.sum(grad_query_pre * query_lin * query_scale, axis=(0, 1))
    gain_key = jnp.sum(grad_key_pre * key_lin * key_scale, axis=(0, 1))
    grad_query_low = (
        norm_back(grad_query_pre, query_lin, query_scale, query_gain)
        .astype(jnp.bfloat16)
        .reshape(tok_count, head_count * head_width)
    )
    grad_key_low = (
        norm_back(grad_key_pre, key_lin, key_scale, key_gain)
        .astype(jnp.bfloat16)
        .reshape(tok_count, kv_count * head_width)
    )
    grad_value_low = grad_values.astype(jnp.bfloat16).reshape(tok_count, kv_count * head_width)
    back_full = (
        jnp.dot(grad_query_low, w_query.T, preferred_element_type=f32)
        + jnp.dot(grad_key_low, w_key.T, preferred_element_type=f32)
        + jnp.dot(grad_value_low, w_value.T, preferred_element_type=f32)
    )
    back_one = back_full.astype(jnp.bfloat16)
    grad_norm_one = scatter_rows(back_one, "tensor")
    gain_one = jnp.sum(back_full * normed_one.astype(f32), axis=0) / attn_gain
    split_one = split_columns(normed_one, "dp")
    grad_w_query = weight_grad(split_one, grad_query_low, "dp", True)
    grad_w_key = weight_grad(split_one, grad_key_low, "dp", False)
    grad_w_value = weight_grad(split_one, grad_value_low, "dp", False)
    grad_input = (
        grad_hidden + norm_back(grad_norm_one, resid, scale_one, attn_gain)
    ).astype(jnp.bfloat16)
    gains = (gain_one, gain_two, gain_query, gain_key)
    packed = total_sum(jnp.concatenate(gains), ("dp", "tensor"))
    ends = []
    at = 0
    for part in gains:
        ends.append(packed[at : at + part.shape[0]])
        at += part.shape[0]
    gain_one, gain_two, gain_query, gain_key = ends
    return (
        block_out,
        grad_input,
        gain_one,
        grad_w_query,
        grad_w_key,
        grad_w_value,
        gain_query,
        gain_key,
        grad_w_output,
        gain_two,
        grad_w_gate,
        grad_w_up,
        grad_down,
    )


def solution(mesh):
    in_specs = (
        P(("dp", "tensor"), None),
        P(),
        P(None, "tensor"),
        P(None, "tensor"),
        P(None, "tensor"),
        P(),
        P(),
        P("tensor", None),
        P(),
        P(None, "tensor"),
        P(None, "tensor"),
        P("tensor", None),
        P(("dp", "tensor"), None),
    )
    out_specs = (
        P(("dp", "tensor"), None),
        P(("dp", "tensor"), None),
        P(),
        P("dp", "tensor"),
        P("dp", "tensor"),
        P("dp", "tensor"),
        P(),
        P(),
        P("tensor", "dp"),
        P(),
        P("dp", "tensor"),
        P("dp", "tensor"),
        P("tensor", "dp"),
    )
    return jax.shard_map(
        on_device, mesh=mesh, in_specs=in_specs, out_specs=out_specs, check_vma=False
    )
```

```python
import jax
import jax.numpy as jnp
from jax import lax
from jax.experimental import pallas as pl
from jax.experimental.pallas import tpu as pltpu
from jax.sharding import PartitionSpec as P


SEQ = 512

EPS = 1e-06
THETA = 1000000.0


def rope_tables(length, head_width):
    half_width = head_width // 2
    inverse_freq = THETA ** (-(jnp.arange(half_width, dtype=jnp.float32) * 2.0 / head_width))
    positions = jnp.arange(length, dtype=jnp.float32)
    angles = positions[:, None] * inverse_freq[None, :]
    return (jnp.cos(angles)[:, None, :], jnp.sin(angles)[:, None, :])


def rope_apply(values, cosine_table, sine_table):
    half_width = values.shape[-1] // 2
    first_half = values[..., :half_width]
    second_half = values[..., half_width:]
    return jnp.concatenate(
        [
            first_half * cosine_table - second_half * sine_table,
            second_half * cosine_table + first_half * sine_table,
        ],
        axis=-1,
    )


def rope_back(grad_rows, cosine_table, sine_table):
    half_width = grad_rows.shape[-1] // 2
    first_half = grad_rows[..., :half_width]
    second_half = grad_rows[..., half_width:]
    return jnp.concatenate(
        [
            first_half * cosine_table + second_half * sine_table,
            second_half * cosine_table - first_half * sine_table,
        ],
        axis=-1,
    )


def row_scale(values):
    return lax.rsqrt(jnp.mean(values * values, axis=-1, keepdims=True) + EPS)


def norm_back(grad_out, values, scale_rows, gain_row):
    weighted = grad_out * gain_row
    inner_mean = jnp.mean(weighted * values, axis=-1, keepdims=True)
    return scale_rows * weighted - values * scale_rows**3 * inner_mean


def causal_scores(grouped, key_seq, factor):
    length = grouped.shape[0]
    scores = (
        jnp.einsum("qgrd,kgd->grqk", grouped, key_seq, preferred_element_type=jnp.float32) * factor
    )
    rows_at = lax.broadcasted_iota(jnp.int32, (length, length), 0)
    cols_at = lax.broadcasted_iota(jnp.int32, (length, length), 1)
    return jnp.where(cols_at <= rows_at, scores, -jnp.inf)


def attend_forward(inputs):
    query_seq, key_seq, value_seq = inputs
    length, head_count, head_width = query_seq.shape
    kv_count = key_seq.shape[1]
    grouped = query_seq.reshape(length, kv_count, head_count // kv_count, head_width)
    scores = causal_scores(grouped, key_seq, head_width ** (-0.5))
    top_score = jnp.max(scores, axis=-1, keepdims=True)
    log_total = top_score + jnp.log(jnp.sum(jnp.exp(scores - top_score), axis=-1, keepdims=True))
    prob_low = jnp.exp(scores - log_total).astype(jnp.bfloat16)
    mixed_seq = jnp.einsum(
        "grqk,kgd->qgrd", prob_low, value_seq, preferred_element_type=jnp.float32
    )
    return (mixed_seq.astype(jnp.bfloat16).reshape(length, head_count, head_width), log_total)


def attend_backward(inputs):
    query_seq, key_seq, value_seq, mixed_seq, log_total, grad_mixed = inputs
    length, head_count, head_width = query_seq.shape
    kv_count = key_seq.shape[1]
    ratio = head_count // kv_count
    factor = head_width ** (-0.5)
    grouped = query_seq.reshape(length, kv_count, ratio, head_width)
    scores = causal_scores(grouped, key_seq, factor)
    prob_full = jnp.exp(scores - log_total)
    prob_low = prob_full.astype(jnp.bfloat16)
    grad_grouped = grad_mixed.reshape(length, kv_count, ratio, head_width)
    inner_rows = jnp.sum(grad_mixed.astype(jnp.float32) * mixed_seq.astype(jnp.float32), axis=-1)
    inner_rows = jnp.transpose(inner_rows.reshape(length, kv_count, ratio), (1, 2, 0))[..., None]
    grad_probs = jnp.einsum(
        "qgrd,kgd->grqk", grad_grouped, value_seq, preferred_element_type=jnp.float32
    )
    grad_scores = (prob_full * (grad_probs - inner_rows)).astype(jnp.bfloat16)
    grad_query = (
        jnp.einsum("grqk,kgd->qgrd", grad_scores, key_seq, preferred_element_type=jnp.float32)
        * factor
    )
    grad_key = (
        jnp.einsum("grqk,qgrd->kgd", grad_scores, grouped, preferred_element_type=jnp.float32)
        * factor
    )
    grad_value = jnp.einsum(
        "grqk,qgrd->kgd", prob_low, grad_grouped, preferred_element_type=jnp.float32
    )
    return (grad_query.reshape(length, head_count, head_width), grad_key, grad_value)


def axis_bits(axis):
    return lax.axis_size(axis).bit_length() - 1


def rotate(values, axis, step):
    count = lax.axis_size(axis)
    return lax.ppermute(values, axis, [(i, (i + step) % count) for i in range(count)])


def gather_rows(values, axis):
    count = lax.axis_size(axis)
    me = lax.axis_index(axis)
    rows = values.shape[0]
    parts = [values] + [rotate(values, axis, step) for step in range(1, count)]
    full = jnp.zeros((count * rows,) + values.shape[1:], values.dtype)
    for step, part in enumerate(parts):
        owner = lax.rem(me - step + count, count)
        full = lax.dynamic_update_slice_in_dim(full, part, owner * rows, 0)
    return full


def scatter_rows(values, axis):
    count = lax.axis_size(axis)
    me = lax.axis_index(axis)
    rows = values.shape[0] // count

    def block(owner):
        return lax.dynamic_slice_in_dim(values, owner * rows, rows, 0)

    got = [
        rotate(block(lax.rem(me + step, count)), axis, step) for step in range(1, count)
    ]
    total = block(me).astype(jnp.float32)
    for part in got:
        total = total + part.astype(jnp.float32)
    return total


def pick_columns(values, axis, which, rising):
    count = lax.axis_size(axis)
    width = values.shape[1] // count
    rest = axis_bits(axis) - 1
    order = list(range(count // 2))
    if rising:
        order = [sum(((j >> i) & 1) << (rest - 1 - i) for i in range(rest)) for j in order]
    return jnp.concatenate(
        [lax.dynamic_slice_in_dim(values, (2 * j + which) * width, width, 1) for j in order],
        axis=1,
    )


def split_columns(values, axis, rising):
    low = lax.rem(lax.axis_index(axis), 2)
    return pick_columns(values, axis, 1 - low, rising), pick_columns(values, axis, low, rising)


def outer(split, right):
    return tuple(
        lax.dot_general(
            side, right, (((0,), (0,)), ((), ())), preferred_element_type=jnp.float32
        ).astype(jnp.bfloat16)
        for side in split
    )


CHUNK = 64


def by_chunks(rows, body):
    size = min(rows, CHUNK)

    @pl.loop(0, rows // size)
    def _(i):
        body(pl.multiple_of(i * size, size), size)


def remote(src, dst, send_sem, recv_sem, axis, peer):
    return pltpu.make_async_remote_copy(
        src_ref=src,
        dst_ref=dst,
        send_sem=send_sem,
        recv_sem=recv_sem,
        device_id={axis: peer},
        device_id_type=pl.DeviceIdType.MESH,
    )


def partner(me, bit):
    mine = lax.rem(me // (1 << bit), 2)
    return me + (1 - 2 * mine) * (1 << bit), mine


class Spread:
    def __init__(self, full, send, recv):
        self.full, self.send, self.recv = full, send, recv
        self.count = lax.axis_size("tensor")
        self.me = lax.axis_index("tensor")
        self.rows = full.shape[0] // self.count
        self.own = pl.ds(pl.multiple_of(self.me * self.rows, self.rows), self.rows)

    def copies(self):
        here = self.full.at[self.own]
        return [
            remote(
                here, here, self.send.at[step - 1], self.recv.at[step - 1],
                "tensor", lax.rem(self.me + step, self.count),
            )
            for step in range(1, self.count)
        ]

    def start(self):
        for copy in self.copies():
            copy.start()

    def wait(self):
        for copy in self.copies():
            copy.wait()


class Collect:
    def __init__(self, part, got, send, recv):
        self.part, self.got, self.send, self.recv = part, got, send, recv
        self.count = lax.axis_size("tensor")
        self.me = lax.axis_index("tensor")
        self.rows = part.shape[0] // self.count

    def copies(self):
        made = []
        for step in range(1, self.count):
            peer = lax.rem(self.me + step, self.count)
            rows = pl.ds(pl.multiple_of(peer * self.rows, self.rows), self.rows)
            made.append(
                remote(
                    self.part.at[rows], self.got.at[step - 1],
                    self.send.at[step - 1], self.recv.at[step - 1], "tensor", peer,
                )
            )
        return made

    def start(self):
        for copy in self.copies():
            copy.start()

    def wait(self):
        for copy in self.copies():
            copy.wait()

    def total(self, at, size):
        own = pl.multiple_of(self.me * self.rows + at, size)
        value = self.part[pl.ds(own, size), :].astype(jnp.float32)
        for step in range(1, self.count):
            value = value + self.got[step - 1, pl.ds(at, size), :].astype(jnp.float32)
        return value


class Halving:
    def __init__(self, away, home, out, rising, got, sent, kept, send, recv):
        bits = axis_bits("dp")
        rest = list(range(1, bits))
        self.bits = [0] + (rest if rising else rest[::-1])
        self.away, self.home, self.out = away, home, out
        self.got, self.sent, self.kept = got, sent, kept
        self.send, self.recv = send, recv
        self.me = lax.axis_index("dp")

    def copy(self, step):
        source = self.away if step == 0 else self.sent[step - 1]
        peer, _ = partner(self.me, self.bits[step])
        return remote(source, self.got[step], self.send.at[step], self.recv.at[step], "dp", peer)

    def start(self):
        self.copy(0).start()

    def advance(self, step):
        self.copy(step).wait()
        keep = self.home if step == 0 else self.kept[step - 1]
        got = self.got[step]
        if step == len(self.bits) - 1:

            def last(at, size):
                here = pl.ds(at, size)
                self.out[here, :] = keep[here, :].astype(jnp.float32) + got[here, :].astype(
                    jnp.float32
                )

            by_chunks(keep.shape[0], last)
            return
        _, mine = partner(self.me, self.bits[step + 1])
        half = keep.shape[0] // 2

        def add(which, target):
            def body(at, size):
                there = pl.ds(pl.multiple_of(which * half + at, size), size)
                total = keep[there, :].astype(jnp.float32) + got[there, :].astype(jnp.float32)
                target[pl.ds(at, size), :] = total.astype(jnp.bfloat16)

            by_chunks(half, body)

        add(1 - mine, self.sent[step])
        self.copy(step + 1).start()
        add(mine, self.kept[step])


class Totals:
    def __init__(self, value, out, sent, got, send, recv):
        self.value, self.out, self.sent, self.got = value, out, sent, got
        self.send, self.recv = send, recv
        self.steps = [(axis, bit) for axis in ("dp", "tensor") for bit in range(axis_bits(axis))]

    def copy(self, step):
        axis, bit = self.steps[step]
        peer, _ = partner(lax.axis_index(axis), bit)
        return remote(
            self.sent.at[step], self.got.at[step], self.send.at[step], self.recv.at[step],
            axis, peer,
        )

    def start(self):
        self.sent[0] = self.value[...]
        self.copy(0).start()

    def advance(self, step):
        self.copy(step).wait()
        total = self.sent[step] + self.got[step]
        if step == len(self.steps) - 1:
            self.out[...] = total
        else:
            self.sent[step + 1] = total
            self.copy(step + 1).start()


def greet(dp):
    barrier = pltpu.get_barrier_semaphore()
    count = lax.axis_size("tensor")
    me = lax.axis_index("tensor")
    peers = [("tensor", lax.rem(me + step, count)) for step in range(1, count)]
    if dp:
        place = lax.axis_index("dp")
        peers += [("dp", partner(place, bit)[0]) for bit in range(axis_bits("dp"))]
    for axis, peer in peers:
        pl.semaphore_signal(
            barrier, inc=1, device_id={axis: peer}, device_id_type=pl.DeviceIdType.MESH
        )
    pl.semaphore_wait(barrier, len(peers))


def sems(count):
    return [pltpu.SemaphoreType.DMA((count,)), pltpu.SemaphoreType.DMA((count,))]


def halving_scratch(home):
    bits = axis_bits("dp")
    rows, width = home.shape
    shapes = [pltpu.VMEM((rows >> s, width), jnp.bfloat16) for s in range(bits)]
    smaller = [pltpu.VMEM((rows >> (s + 1), width), jnp.bfloat16) for s in range(bits - 1)]
    return shapes + smaller + smaller + sems(bits)


def take_halving(away, home, out, rising, refs):
    bits = axis_bits("dp")
    got, refs = refs[:bits], refs[bits:]
    sent, refs = refs[: bits - 1], refs[bits - 1 :]
    kept, refs = refs[: bits - 1], refs[bits - 1 :]
    return Halving(away, home, out, rising, got, sent, kept, *refs)


def halving_size():
    return axis_bits("dp") * 3


def collect_scratch(part):
    count = lax.axis_size("tensor")
    return [
        pltpu.VMEM((count - 1, part.shape[0] // count, part.shape[1]), jnp.bfloat16)
    ] + sems(count - 1)


def call(kernel, name, ident, out_shape, scratch, args):
    vmem = pl.BlockSpec(memory_space=pltpu.VMEM)
    return pl.pallas_call(
        kernel,
        name=name,
        out_shape=out_shape,
        in_specs=[vmem] * len(args),
        out_specs=[vmem] * len(out_shape),
        scratch_shapes=scratch,
        compiler_params=pltpu.CompilerParams(collective_id=ident, has_side_effects=True),
    )(*args)


def spread_rows(tokens, gain):
    rows, width = tokens.shape
    count = lax.axis_size("tensor")

    def kernel(tokens_ref, gain_ref, full_ref, send, recv):
        out = Spread(full_ref, send, recv)

        def body(at, size):
            here = pl.ds(at, size)
            value = tokens_ref[here, :].astype(jnp.float32)
            full_ref[pl.ds(pl.multiple_of(out.me * rows + at, size), size), :] = (
                value * row_scale(value) * gain_ref[...]
            ).astype(jnp.bfloat16)

        by_chunks(rows, body)
        greet(False)
        out.start()
        out.wait()

    full = jax.ShapeDtypeStruct((rows * count, width), jnp.bfloat16)
    return call(
        kernel, "spread_rows", 1, [full], sems(count - 1), (tokens, gain[None, :])
    )[0]


def finish_attention(part, tokens, gain):
    rows, width = tokens.shape
    count = lax.axis_size("tensor")

    def kernel(part_ref, tokens_ref, gain_ref, hidden_ref, full_ref, got, send, recv, send2, recv2):
        total = Collect(part_ref, got, send, recv)
        out = Spread(full_ref, send2, recv2)
        greet(False)
        total.start()
        total.wait()

        def body(at, size):
            here = pl.ds(at, size)
            value = tokens_ref[here, :].astype(jnp.float32) + total.total(at, size)
            hidden_ref[here, :] = value
            full_ref[pl.ds(pl.multiple_of(out.me * rows + at, size), size), :] = (
                value * row_scale(value) * gain_ref[...]
            ).astype(jnp.bfloat16)

        by_chunks(rows, body)
        out.start()
        out.wait()

    shapes = [
        jax.ShapeDtypeStruct((rows, width), jnp.float32),
        jax.ShapeDtypeStruct((rows * count, width), jnp.bfloat16),
    ]
    scratch = collect_scratch(part) + sems(count - 1)
    return call(
        kernel, "finish_attention", 2, shapes, scratch, (part, tokens, gain[None, :])
    )


def finish_mlp_back(part, hidden, cotangent, gain, grads, rising):
    rows, width = hidden.shape
    count = lax.axis_size("tensor")
    pairs = len(grads)
    bits = axis_bits("dp")
    block = grads[0][1].shape[0] >> (bits - 1)

    def kernel(*refs):
        part_ref, hidden_ref, cot_ref, gain_ref = refs[:4]
        sides, refs = refs[4 : 4 + 2 * pairs], refs[4 + 2 * pairs :]
        grad_ref, full_ref, norm_ref = refs[:3]
        outs, refs = refs[3 : 3 + pairs], refs[3 + pairs :]
        total = Collect(part_ref, *refs[:3])
        out = Spread(full_ref, *refs[3:5])
        refs = refs[5:]
        size_of = halving_size()
        sums = [
            take_halving(
                sides[2 * i], sides[2 * i + 1], outs[i], rising[i],
                refs[i * size_of : (i + 1) * size_of],
            )
            for i in range(pairs)
        ]
        greet(True)
        total.start()
        for item in sums:
            item.start()
        for item in sums:
            item.advance(0)
        total.wait()

        def body(at, size):
            here = pl.ds(at, size)
            grad = total.total(at, size)
            value = hidden_ref[here, :]
            norm_ref[here, :] = grad
            result = cot_ref[here, :].astype(jnp.float32) + norm_back(
                grad, value, row_scale(value), gain_ref[...]
            )
            grad_ref[here, :] = result
            full_ref[pl.ds(pl.multiple_of(out.me * rows + at, size), size), :] = result.astype(
                jnp.bfloat16
            )

        by_chunks(rows, body)
        out.start()
        for step in range(1, bits):
            for item in sums:
                item.advance(step)
        out.wait()

    shapes = [
        jax.ShapeDtypeStruct((rows, width), jnp.float32),
        jax.ShapeDtypeStruct((rows * count, width), jnp.bfloat16),
        jax.ShapeDtypeStruct((rows, width), jnp.float32),
    ] + [jax.ShapeDtypeStruct((block, home.shape[1]), jnp.float32) for _, home in grads]
    scratch = collect_scratch(part) + sems(count - 1)
    for _, home in grads:
        scratch += halving_scratch(home)
    args = (part, hidden, cotangent, gain[None, :]) + tuple(x for pair in grads for x in pair)
    return call(kernel, "finish_mlp_back", 3, shapes, scratch, args)


def finish_all(part, packed, grads, rising):
    count = lax.axis_size("tensor")
    rows, width = part.shape[0] // count, part.shape[1]
    pairs = len(grads)
    bits = axis_bits("dp")
    block = grads[0][1].shape[0] >> (bits - 1)
    steps = bits + axis_bits("tensor")

    def kernel(*refs):
        part_ref, packed_ref = refs[:2]
        sides, refs = refs[2 : 2 + 2 * pairs], refs[2 + 2 * pairs :]
        norm_ref, packed_out = refs[:2]
        outs, refs = refs[2 : 2 + pairs], refs[2 + pairs :]
        total = Collect(part_ref, *refs[:3])
        small = Totals(packed_ref, packed_out, *refs[3:7])
        refs = refs[7:]
        size_of = halving_size()
        sums = [
            take_halving(
                sides[2 * i], sides[2 * i + 1], outs[i], rising[i],
                refs[i * size_of : (i + 1) * size_of],
            )
            for i in range(pairs)
        ]
        greet(True)
        small.start()
        total.start()
        for item in sums:
            item.start()
        done = 0
        for step in range(bits):
            for item in sums:
                item.advance(step)
            small.advance(done)
            done += 1
        while done < steps:
            small.advance(done)
            done += 1
        total.wait()

        def body(at, size):
            norm_ref[pl.ds(at, size), :] = total.total(at, size)

        by_chunks(rows, body)

    shapes = [
        jax.ShapeDtypeStruct((rows, width), jnp.float32),
        jax.ShapeDtypeStruct(packed.shape, jnp.float32),
    ] + [jax.ShapeDtypeStruct((block, home.shape[1]), jnp.float32) for _, home in grads]
    scratch = collect_scratch(part)
    scratch += [pltpu.VMEM((steps,) + packed.shape, jnp.float32)] * 2 + sems(steps)
    for _, home in grads:
        scratch += halving_scratch(home)
    args = (part, packed) + tuple(x for pair in grads for x in pair)
    return call(kernel, "finish_all", 4, shapes, scratch, args)


def on_device(
    tokens_in,
    attn_gain,
    w_query,
    w_key,
    w_value,
    query_gain,
    key_gain,
    w_output,
    mlp_gain,
    w_gate,
    w_up,
    w_down,
    out_cotangent,
):
    f32 = jnp.float32
    head_width = query_gain.shape[0]
    head_count = w_query.shape[1] // head_width
    kv_count = w_key.shape[1] // head_width
    cosine_table, sine_table = rope_tables(SEQ, head_width)
    resid = tokens_in.astype(f32)
    scale_one = row_scale(resid)
    normed_one = spread_rows(tokens_in, attn_gain)
    normed_one, cotangent = lax.optimization_barrier((normed_one, out_cotangent))
    grad_all = gather_rows(cotangent, "tensor")
    tok_count = normed_one.shape[0]
    seq_count = tok_count // SEQ
    query_lin = jnp.dot(normed_one, w_query, preferred_element_type=f32).reshape(
        tok_count, head_count, head_width
    )
    key_lin = jnp.dot(normed_one, w_key, preferred_element_type=f32).reshape(
        tok_count, kv_count, head_width
    )
    value_heads = (
        jnp.dot(normed_one, w_value, preferred_element_type=f32)
        .astype(jnp.bfloat16)
        .reshape(seq_count, SEQ, kv_count, head_width)
    )
    query_scale = row_scale(query_lin)
    key_scale = row_scale(key_lin)
    query_rot = rope_apply(
        (query_lin * query_scale * query_gain).reshape(seq_count, SEQ, head_count, head_width),
        cosine_table,
        sine_table,
    ).astype(jnp.bfloat16)
    key_rot = rope_apply(
        (key_lin * key_scale * key_gain).reshape(seq_count, SEQ, kv_count, head_width),
        cosine_table,
        sine_table,
    ).astype(jnp.bfloat16)
    mixed_heads, log_totals = lax.map(attend_forward, (query_rot, key_rot, value_heads))
    attn_flat = mixed_heads.reshape(tok_count, head_count * head_width)
    attn_part = jnp.dot(attn_flat, w_output, preferred_element_type=f32).astype(jnp.bfloat16)
    attn_part, grad_all = lax.optimization_barrier((attn_part, grad_all))
    hidden, normed_two = finish_attention(attn_part, tokens_in, mlp_gain)
    scale_two = row_scale(hidden)
    gate_lin = jnp.dot(normed_two, w_gate, preferred_element_type=f32)
    up_lin = jnp.dot(normed_two, w_up, preferred_element_type=f32)
    gate_sig = jax.nn.sigmoid(gate_lin)
    activated = (gate_lin * gate_sig * up_lin).astype(jnp.bfloat16)
    grad_act = jnp.dot(grad_all, w_down.T, preferred_element_type=f32)
    grad_gate = (grad_act * up_lin * gate_sig * (1.0 + gate_lin * (1.0 - gate_sig))).astype(
        jnp.bfloat16
    )
    grad_up = (grad_act * gate_lin * gate_sig).astype(jnp.bfloat16)
    back_two = (
        jnp.dot(grad_gate, w_gate.T, preferred_element_type=f32)
        + jnp.dot(grad_up, w_up.T, preferred_element_type=f32)
    ).astype(jnp.bfloat16)
    two_rising = split_columns(normed_two, "dp", True)
    two_falling = split_columns(normed_two, "dp", False)
    first_grads = (
        outer(two_rising, grad_gate),
        outer(two_falling, grad_up),
        outer(split_columns(grad_all, "dp", True), activated),
    )
    grad_hidden, grad_hidden_low, grad_norm_two, grad_w_gate, grad_w_up, grad_down = (
        finish_mlp_back(
            back_two, hidden, out_cotangent, mlp_gain, first_grads, (True, False, True)
        )
    )
    grad_down = grad_down.T
    gain_two = jnp.sum(grad_norm_two * hidden * scale_two, axis=0)
    activated_late, grad_hidden_low = lax.optimization_barrier((activated, grad_hidden_low))
    mlp_part = jnp.dot(activated_late, w_down, preferred_element_type=f32).astype(jnp.bfloat16)
    mlp_sum = scatter_rows(mlp_part, "tensor")
    block_out = (hidden + mlp_sum).astype(jnp.bfloat16)
    output_pair = outer(split_columns(grad_hidden_low, "dp", False), attn_flat)
    grad_mixed = (
        jnp.dot(grad_hidden_low, w_output.T, preferred_element_type=f32)
        .astype(jnp.bfloat16)
        .reshape(seq_count, SEQ, head_count, head_width)
    )
    grad_query_rot, grad_key_rot, grad_values = lax.map(
        attend_backward, (query_rot, key_rot, value_heads, mixed_heads, log_totals, grad_mixed)
    )
    grad_query_pre = rope_back(grad_query_rot, cosine_table, sine_table).reshape(
        tok_count, head_count, head_width
    )
    grad_key_pre = rope_back(grad_key_rot, cosine_table, sine_table).reshape(
        tok_count, kv_count, head_width
    )
    gain_query = jnp.sum(grad_query_pre * query_lin * query_scale, axis=(0, 1))
    gain_key = jnp.sum(grad_key_pre * key_lin * key_scale, axis=(0, 1))
    grad_query_low = (
        norm_back(grad_query_pre, query_lin, query_scale, query_gain)
        .astype(jnp.bfloat16)
        .reshape(tok_count, head_count * head_width)
    )
    grad_key_low = (
        norm_back(grad_key_pre, key_lin, key_scale, key_gain)
        .astype(jnp.bfloat16)
        .reshape(tok_count, kv_count * head_width)
    )
    grad_value_low = grad_values.astype(jnp.bfloat16).reshape(tok_count, kv_count * head_width)
    back_full = (
        jnp.dot(grad_query_low, w_query.T, preferred_element_type=f32)
        + jnp.dot(grad_key_low, w_key.T, preferred_element_type=f32)
        + jnp.dot(grad_value_low, w_value.T, preferred_element_type=f32)
    )
    back_one = back_full.astype(jnp.bfloat16)
    gain_one = jnp.sum(back_full * normed_one.astype(f32), axis=0) / attn_gain
    one_rising = split_columns(normed_one, "dp", True)
    one_falling = split_columns(normed_one, "dp", False)
    last_grads = (
        outer(one_rising, grad_query_low),
        output_pair,
        outer(one_falling, grad_key_low),
        outer(one_rising, grad_value_low),
    )
    gains = (gain_one, gain_two, gain_query, gain_key)
    packed = jnp.concatenate(gains)
    lanes = query_gain.shape[0]
    short = -packed.shape[0] % (8 * lanes)
    packed = jnp.pad(packed, (0, short)).reshape(-1, lanes)
    back_one, block_out = lax.optimization_barrier((back_one, block_out))
    grad_norm_one, packed, grad_w_query, grad_w_output, grad_w_key, grad_w_value = finish_all(
        back_one, packed, last_grads, (True, False, False, True)
    )
    grad_w_output = grad_w_output.T
    packed = packed.reshape(-1)
    grad_input = (
        grad_hidden + norm_back(grad_norm_one, resid, scale_one, attn_gain)
    ).astype(jnp.bfloat16)
    ends = []
    at = 0
    for part in gains:
        ends.append(packed[at : at + part.shape[0]])
        at += part.shape[0]
    gain_one, gain_two, gain_query, gain_key = ends
    return (
        block_out,
        grad_input,
        gain_one,
        grad_w_query,
        grad_w_key,
        grad_w_value,
        gain_query,
        gain_key,
        grad_w_output,
        gain_two,
        grad_w_gate,
        grad_w_up,
        grad_down,
    )


def solution(mesh):
    in_specs = (
        P(("dp", "tensor"), None),
        P(),
        P(None, "tensor"),
        P(None, "tensor"),
        P(None, "tensor"),
        P(),
        P(),
        P("tensor", None),
        P(),
        P(None, "tensor"),
        P(None, "tensor"),
        P("tensor", None),
        P(("dp", "tensor"), None),
    )
    out_specs = (
        P(("dp", "tensor"), None),
        P(("dp", "tensor"), None),
        P(),
        P("dp", "tensor"),
        P("dp", "tensor"),
        P("dp", "tensor"),
        P(),
        P(),
        P("tensor", "dp"),
        P(),
        P("dp", "tensor"),
        P("dp", "tensor"),
        P("tensor", "dp"),
    )
    return jax.shard_map(
        on_device, mesh=mesh, in_specs=in_specs, out_specs=out_specs, check_vma=False
    )
```

```python
import jax
import jax.numpy as jnp
from jax import lax
from jax.experimental import pallas as pl
from jax.experimental.pallas import tpu as pltpu
from jax.sharding import PartitionSpec as P


SEQ = 512

EPS = 1e-06
THETA = 1000000.0


def rope_tables(length, head_width):
    half_width = head_width // 2
    inverse_freq = THETA ** (-(jnp.arange(half_width, dtype=jnp.float32) * 2.0 / head_width))
    positions = jnp.arange(length, dtype=jnp.float32)
    angles = positions[:, None] * inverse_freq[None, :]
    return (jnp.cos(angles)[:, None, :], jnp.sin(angles)[:, None, :])


def rope_apply(values, cosine_table, sine_table):
    half_width = values.shape[-1] // 2
    first_half = values[..., :half_width]
    second_half = values[..., half_width:]
    return jnp.concatenate(
        [
            first_half * cosine_table - second_half * sine_table,
            second_half * cosine_table + first_half * sine_table,
        ],
        axis=-1,
    )


def rope_back(grad_rows, cosine_table, sine_table):
    half_width = grad_rows.shape[-1] // 2
    first_half = grad_rows[..., :half_width]
    second_half = grad_rows[..., half_width:]
    return jnp.concatenate(
        [
            first_half * cosine_table + second_half * sine_table,
            second_half * cosine_table - first_half * sine_table,
        ],
        axis=-1,
    )


def row_scale(values):
    return lax.rsqrt(jnp.mean(values * values, axis=-1, keepdims=True) + EPS)


def norm_back(grad_out, values, scale_rows, gain_row):
    weighted = grad_out * gain_row
    inner_mean = jnp.mean(weighted * values, axis=-1, keepdims=True)
    return scale_rows * weighted - values * scale_rows**3 * inner_mean


def causal_scores(grouped, key_seq, factor):
    length = grouped.shape[0]
    scores = (
        jnp.einsum("qgrd,kgd->grqk", grouped, key_seq, preferred_element_type=jnp.float32) * factor
    )
    rows_at = lax.broadcasted_iota(jnp.int32, (length, length), 0)
    cols_at = lax.broadcasted_iota(jnp.int32, (length, length), 1)
    return jnp.where(cols_at <= rows_at, scores, -jnp.inf)


def attend_forward(inputs):
    query_seq, key_seq, value_seq = inputs
    length, head_count, head_width = query_seq.shape
    kv_count = key_seq.shape[1]
    grouped = query_seq.reshape(length, kv_count, head_count // kv_count, head_width)
    scores = causal_scores(grouped, key_seq, head_width ** (-0.5))
    top_score = jnp.max(scores, axis=-1, keepdims=True)
    log_total = top_score + jnp.log(jnp.sum(jnp.exp(scores - top_score), axis=-1, keepdims=True))
    prob_low = jnp.exp(scores - log_total).astype(jnp.bfloat16)
    mixed_seq = jnp.einsum(
        "grqk,kgd->qgrd", prob_low, value_seq, preferred_element_type=jnp.float32
    )
    return (mixed_seq.astype(jnp.bfloat16).reshape(length, head_count, head_width), log_total)


def attend_backward(inputs):
    query_seq, key_seq, value_seq, mixed_seq, log_total, grad_mixed = inputs
    length, head_count, head_width = query_seq.shape
    kv_count = key_seq.shape[1]
    ratio = head_count // kv_count
    factor = head_width ** (-0.5)
    grouped = query_seq.reshape(length, kv_count, ratio, head_width)
    scores = causal_scores(grouped, key_seq, factor)
    prob_full = jnp.exp(scores - log_total)
    prob_low = prob_full.astype(jnp.bfloat16)
    grad_grouped = grad_mixed.reshape(length, kv_count, ratio, head_width)
    inner_rows = jnp.sum(grad_mixed.astype(jnp.float32) * mixed_seq.astype(jnp.float32), axis=-1)
    inner_rows = jnp.transpose(inner_rows.reshape(length, kv_count, ratio), (1, 2, 0))[..., None]
    grad_probs = jnp.einsum(
        "qgrd,kgd->grqk", grad_grouped, value_seq, preferred_element_type=jnp.float32
    )
    grad_scores = (prob_full * (grad_probs - inner_rows)).astype(jnp.bfloat16)
    grad_query = (
        jnp.einsum("grqk,kgd->qgrd", grad_scores, key_seq, preferred_element_type=jnp.float32)
        * factor
    )
    grad_key = (
        jnp.einsum("grqk,qgrd->kgd", grad_scores, grouped, preferred_element_type=jnp.float32)
        * factor
    )
    grad_value = jnp.einsum(
        "grqk,qgrd->kgd", prob_low, grad_grouped, preferred_element_type=jnp.float32
    )
    return (grad_query.reshape(length, head_count, head_width), grad_key, grad_value)


def axis_bits(axis):
    return lax.axis_size(axis).bit_length() - 1


def rotate(values, axis, step):
    count = lax.axis_size(axis)
    return lax.ppermute(values, axis, [(i, (i + step) % count) for i in range(count)])


def gather_rows(values, axis):
    count = lax.axis_size(axis)
    me = lax.axis_index(axis)
    parts = [values] + [rotate(values, axis, step) for step in range(1, count)]
    return jnp.concatenate(
        [lax.select_n(lax.rem(me - place + count, count), *parts) for place in range(count)]
    )


def scatter_rows(values, axis):
    count = lax.axis_size(axis)
    me = lax.axis_index(axis)
    rows = values.shape[0] // count

    def block(owner):
        return lax.dynamic_slice_in_dim(values, owner * rows, rows, 0)

    got = [
        rotate(block(lax.rem(me + step, count)), axis, step) for step in range(1, count)
    ]
    total = block(me).astype(jnp.float32)
    for part in got:
        total = total + part.astype(jnp.float32)
    return total


def pick_columns(values, axis, which, rising):
    count = lax.axis_size(axis)
    width = values.shape[1] // count
    rest = axis_bits(axis) - 1
    order = list(range(count // 2))
    if rising:
        order = [sum(((j >> i) & 1) << (rest - 1 - i) for i in range(rest)) for j in order]
    return jnp.concatenate(
        [lax.dynamic_slice_in_dim(values, (2 * j + which) * width, width, 1) for j in order],
        axis=1,
    )


def split_columns(values, axis, rising):
    low = lax.rem(lax.axis_index(axis), 2)
    return pick_columns(values, axis, 1 - low, rising), pick_columns(values, axis, low, rising)


def outer(split, right):
    return tuple(
        lax.dot_general(
            side, right, (((0,), (0,)), ((), ())), preferred_element_type=jnp.float32
        ).astype(jnp.bfloat16)
        for side in split
    )


CHUNK = 64


def by_chunks(rows, body):
    size = min(rows, CHUNK)

    @pl.loop(0, rows // size)
    def _(i):
        body(pl.multiple_of(i * size, size), size)


def remote(src, dst, send_sem, recv_sem, axis, peer):
    return pltpu.make_async_remote_copy(
        src_ref=src,
        dst_ref=dst,
        send_sem=send_sem,
        recv_sem=recv_sem,
        device_id={axis: peer},
        device_id_type=pl.DeviceIdType.MESH,
    )


def partner(me, bit):
    mine = lax.rem(me // (1 << bit), 2)
    return me + (1 - 2 * mine) * (1 << bit), mine


def lanes_of_line():
    count = lax.axis_size("tensor")
    me = lax.axis_index("tensor")
    near = (2 * me) // count
    first = (near, 1 - 2 * near, me + near * (count - 1 - 2 * me))
    second = (1 - near, 2 * near - 1, count - 1 - first[2])
    return me, count, (first, second)


class Spread:
    def __init__(self, full, send, recv):
        self.full, self.send, self.recv = full, send, recv
        self.me, self.count, self.ways = lanes_of_line()
        self.rows = full.shape[0] // self.count

    def copy(self, way, source):
        flag, step, _ = way
        owner = source + flag * (self.count - 1 - 2 * source)
        there = self.full.at[pl.ds(pl.multiple_of(owner * self.rows, self.rows), self.rows)]
        return remote(
            there, there, self.send.at[flag, source], self.recv.at[flag, source],
            "tensor", lax.rem(self.me + step + self.count, self.count),
        )

    def start(self):
        for way in self.ways:

            @pl.when(way[2] < self.count - 1)
            def _():
                self.copy(way, way[2]).start()

    def forward(self, back):
        for way in self.ways:

            @pl.when(way[2] >= back)
            def _():
                self.copy(way, way[2] - back).wait_recv()

                @pl.when(way[2] < self.count - 1)
                def _():
                    self.copy(way, way[2] - back).start()

    def drain(self):
        for back in range(self.count):
            for way in self.ways:

                @pl.when((way[2] >= back) & (way[2] < self.count - 1))
                def _():
                    self.copy(way, way[2] - back).wait_send()


class Collect:
    def __init__(self, part, got, sent, send, recv):
        self.part, self.got, self.sent, self.send, self.recv = part, got, sent, send, recv
        self.me, self.count, self.ways = lanes_of_line()
        self.rows = part.shape[0] // self.count

    def target(self, way, place):
        owner = place + way[0] * (self.count - 1 - 2 * place)
        return pl.multiple_of(owner * self.rows, self.rows)

    def copy(self, way, place, source):
        flag, step, _ = way
        return remote(
            source, self.got.at[flag, place], self.send.at[flag, place],
            self.recv.at[flag, place], "tensor",
            lax.rem(self.me + step + self.count, self.count),
        )

    def start(self):
        for place in range(self.count - 1, 0, -1):
            for way in self.ways:

                @pl.when(way[2] == 0)
                def _():
                    rows = pl.ds(self.target(way, place), self.rows)
                    self.copy(way, place, self.part.at[rows]).start()

    def relay(self, place):
        for way in self.ways:

            @pl.when((way[2] > 0) & (way[2] < place))
            def _():
                flag = way[0]
                self.copy(way, place, self.sent.at[flag, place]).wait_recv()
                base = self.target(way, place)

                def body(at, size):
                    own = pl.ds(pl.multiple_of(base + at, size), size)
                    here = pl.ds(at, size)
                    total = self.part[own, :].astype(jnp.float32) + self.got[
                        flag, place, here, :
                    ].astype(jnp.float32)
                    self.sent[flag, place, here, :] = total.astype(jnp.bfloat16)

                by_chunks(self.rows, body)
                self.copy(way, place, self.sent.at[flag, place]).start()

            @pl.when((way[2] > 0) & (way[2] == place))
            def _():
                self.copy(way, place, self.sent.at[way[0], place]).wait_recv()

    def drain(self):
        for place in range(self.count - 1, 0, -1):
            for way in self.ways:

                @pl.when(way[2] < place)
                def _():
                    self.copy(way, place, self.sent.at[way[0], place]).wait_send()

    def finish(self, write):
        (first, _, place), (second, _, _) = self.ways
        far = self.count - 1 - place

        def value(at, size):
            own = pl.multiple_of(self.me * self.rows + at, size)
            return self.part[pl.ds(own, size), :].astype(jnp.float32) + self.got[
                second, far, pl.ds(at, size), :
            ].astype(jnp.float32)

        @pl.when(place > 0)
        def _():
            by_chunks(
                self.rows,
                lambda at, size: write(
                    at, size,
                    value(at, size)
                    + self.got[first, place, pl.ds(at, size), :].astype(jnp.float32),
                ),
            )

        @pl.when(place == 0)
        def _():
            by_chunks(self.rows, lambda at, size: write(at, size, value(at, size)))


class Halving:
    def __init__(self, away, home, out, rising, got, sent, kept, send, recv):
        bits = axis_bits("dp")
        rest = list(range(1, bits))
        self.bits = [0] + (rest if rising else rest[::-1])
        self.away, self.home, self.out = away, home, out
        self.got, self.sent, self.kept = got, sent, kept
        self.send, self.recv = send, recv
        self.me = lax.axis_index("dp")

    def copy(self, step):
        source = self.away if step == 0 else self.sent[step - 1]
        peer, _ = partner(self.me, self.bits[step])
        return remote(source, self.got[step], self.send.at[step], self.recv.at[step], "dp", peer)

    def start(self):
        self.copy(0).start()

    def advance(self, step):
        self.copy(step).wait()
        keep = self.home if step == 0 else self.kept[step - 1]
        got = self.got[step]
        if step == len(self.bits) - 1:

            def last(at, size):
                here = pl.ds(at, size)
                self.out[here, :] = keep[here, :].astype(jnp.float32) + got[here, :].astype(
                    jnp.float32
                )

            by_chunks(keep.shape[0], last)
            return
        _, mine = partner(self.me, self.bits[step + 1])
        half = keep.shape[0] // 2

        def add(which, target):
            def body(at, size):
                there = pl.ds(pl.multiple_of(which * half + at, size), size)
                total = keep[there, :].astype(jnp.float32) + got[there, :].astype(jnp.float32)
                target[pl.ds(at, size), :] = total.astype(jnp.bfloat16)

            by_chunks(half, body)

        add(1 - mine, self.sent[step])
        self.copy(step + 1).start()
        add(mine, self.kept[step])


class Totals:
    def __init__(self, value, out, sent, got, send, recv):
        self.value, self.out, self.sent, self.got = value, out, sent, got
        self.send, self.recv = send, recv
        self.steps = [(axis, bit) for axis in ("dp", "tensor") for bit in range(axis_bits(axis))]

    def copy(self, step):
        axis, bit = self.steps[step]
        peer, _ = partner(lax.axis_index(axis), bit)
        return remote(
            self.sent.at[step], self.got.at[step], self.send.at[step], self.recv.at[step],
            axis, peer,
        )

    def start(self):
        self.sent[0] = self.value[...]
        self.copy(0).start()

    def advance(self, step):
        self.copy(step).wait()
        total = self.sent[step] + self.got[step]
        if step == len(self.steps) - 1:
            self.out[...] = total
        else:
            self.sent[step + 1] = total
            self.copy(step + 1).start()


def greet(dp):
    barrier = pltpu.get_barrier_semaphore()
    count = lax.axis_size("tensor")
    me = lax.axis_index("tensor")
    peers = [("tensor", lax.rem(me + step, count)) for step in range(1, count)]
    if dp:
        place = lax.axis_index("dp")
        peers += [("dp", partner(place, bit)[0]) for bit in range(axis_bits("dp"))]
    for axis, peer in peers:
        pl.semaphore_signal(
            barrier, inc=1, device_id={axis: peer}, device_id_type=pl.DeviceIdType.MESH
        )
    pl.semaphore_wait(barrier, len(peers))


def sems(count):
    return [pltpu.SemaphoreType.DMA((count,)), pltpu.SemaphoreType.DMA((count,))]


def line_sems():
    shape = (2, lax.axis_size("tensor"))
    return [pltpu.SemaphoreType.DMA(shape), pltpu.SemaphoreType.DMA(shape)]


def halving_scratch(home):
    bits = axis_bits("dp")
    rows, width = home.shape
    shapes = [pltpu.VMEM((rows >> s, width), jnp.bfloat16) for s in range(bits)]
    smaller = [pltpu.VMEM((rows >> (s + 1), width), jnp.bfloat16) for s in range(bits - 1)]
    return shapes + smaller + smaller + sems(bits)


def take_halving(away, home, out, rising, refs):
    bits = axis_bits("dp")
    got, refs = refs[:bits], refs[bits:]
    sent, refs = refs[: bits - 1], refs[bits - 1 :]
    kept, refs = refs[: bits - 1], refs[bits - 1 :]
    return Halving(away, home, out, rising, got, sent, kept, *refs)


def halving_size():
    return axis_bits("dp") * 3


def collect_scratch(part):
    count = lax.axis_size("tensor")
    block = pltpu.VMEM((2, count, part.shape[0] // count, part.shape[1]), jnp.bfloat16)
    return [block, block] + line_sems()


def interleave(line, places, sums=(), steps=()):
    places, steps = list(places), list(steps)
    for i in range(max(len(places), len(steps))):
        if i < len(places):
            line(places[i])
        if i < len(steps):
            for item in sums:
                item.advance(steps[i])


def call(kernel, ident, out_shape, scratch, args):
    vmem = pl.BlockSpec(memory_space=pltpu.VMEM)
    return pl.pallas_call(
        kernel,
        out_shape=out_shape,
        in_specs=[vmem] * len(args),
        out_specs=[vmem] * len(out_shape),
        scratch_shapes=scratch,
        compiler_params=pltpu.CompilerParams(collective_id=ident, has_side_effects=True),
    )(*args)


def spread_rows(tokens, gain):
    rows, width = tokens.shape
    count = lax.axis_size("tensor")

    def kernel(tokens_ref, gain_ref, full_ref, send, recv):
        out = Spread(full_ref, send, recv)

        def body(at, size):
            here = pl.ds(at, size)
            value = tokens_ref[here, :].astype(jnp.float32)
            full_ref[pl.ds(pl.multiple_of(out.me * rows + at, size), size), :] = (
                value * row_scale(value) * gain_ref[...]
            ).astype(jnp.bfloat16)

        by_chunks(rows, body)
        greet(False)
        out.start()
        interleave(out.forward, range(1, count))
        out.drain()

    full = jax.ShapeDtypeStruct((rows * count, width), jnp.bfloat16)
    return call(kernel, 1, [full], line_sems(), (tokens, gain[None, :]))[0]


def finish_attention(part, tokens, gain):
    rows, width = tokens.shape
    count = lax.axis_size("tensor")

    def kernel(part_ref, tokens_ref, gain_ref, hidden_ref, full_ref, *refs):
        total = Collect(part_ref, *refs[:4])
        out = Spread(full_ref, *refs[4:])
        greet(False)
        total.start()
        interleave(total.relay, range(count - 1, 0, -1))

        def body(at, size, value):
            here = pl.ds(at, size)
            value = tokens_ref[here, :].astype(jnp.float32) + value
            hidden_ref[here, :] = value
            full_ref[pl.ds(pl.multiple_of(out.me * rows + at, size), size), :] = (
                value * row_scale(value) * gain_ref[...]
            ).astype(jnp.bfloat16)

        total.finish(body)
        out.start()
        interleave(out.forward, range(1, count))
        total.drain()
        out.drain()

    shapes = [
        jax.ShapeDtypeStruct((rows, width), jnp.float32),
        jax.ShapeDtypeStruct((rows * count, width), jnp.bfloat16),
    ]
    scratch = collect_scratch(part) + line_sems()
    return call(kernel, 2, shapes, scratch, (part, tokens, gain[None, :]))


def finish_mlp_back(part, hidden, cotangent, gain, grads, rising):
    rows, width = hidden.shape
    count = lax.axis_size("tensor")
    pairs = len(grads)
    bits = axis_bits("dp")
    block = grads[0][1].shape[0] >> (bits - 1)

    def kernel(*refs):
        part_ref, hidden_ref, cot_ref, gain_ref = refs[:4]
        sides, refs = refs[4 : 4 + 2 * pairs], refs[4 + 2 * pairs :]
        grad_ref, full_ref, norm_ref = refs[:3]
        outs, refs = refs[3 : 3 + pairs], refs[3 + pairs :]
        total = Collect(part_ref, *refs[:4])
        out = Spread(full_ref, *refs[4:6])
        refs = refs[6:]
        size_of = halving_size()
        sums = [
            take_halving(
                sides[2 * i], sides[2 * i + 1], outs[i], rising[i],
                refs[i * size_of : (i + 1) * size_of],
            )
            for i in range(pairs)
        ]
        greet(True)
        total.start()
        for item in sums:
            item.start()
        interleave(total.relay, range(count - 1, 0, -1), sums, range(1))

        def body(at, size, grad):
            here = pl.ds(at, size)
            value = hidden_ref[here, :]
            norm_ref[here, :] = grad
            result = cot_ref[here, :].astype(jnp.float32) + norm_back(
                grad, value, row_scale(value), gain_ref[...]
            )
            grad_ref[here, :] = result
            full_ref[pl.ds(pl.multiple_of(out.me * rows + at, size), size), :] = result.astype(
                jnp.bfloat16
            )

        total.finish(body)
        out.start()
        interleave(out.forward, range(1, count), sums, range(1, bits))
        total.drain()
        out.drain()

    shapes = [
        jax.ShapeDtypeStruct((rows, width), jnp.float32),
        jax.ShapeDtypeStruct((rows * count, width), jnp.bfloat16),
        jax.ShapeDtypeStruct((rows, width), jnp.float32),
    ] + [jax.ShapeDtypeStruct((block, home.shape[1]), jnp.float32) for _, home in grads]
    scratch = collect_scratch(part) + line_sems()
    for _, home in grads:
        scratch += halving_scratch(home)
    args = (part, hidden, cotangent, gain[None, :]) + tuple(x for pair in grads for x in pair)
    return call(kernel, 3, shapes, scratch, args)


def finish_all(part, packed, grads, rising):
    count = lax.axis_size("tensor")
    rows, width = part.shape[0] // count, part.shape[1]
    pairs = len(grads)
    bits = axis_bits("dp")
    block = grads[0][1].shape[0] >> (bits - 1)
    steps = bits + axis_bits("tensor")

    def kernel(*refs):
        part_ref, packed_ref = refs[:2]
        sides, refs = refs[2 : 2 + 2 * pairs], refs[2 + 2 * pairs :]
        norm_ref, packed_out = refs[:2]
        outs, refs = refs[2 : 2 + pairs], refs[2 + pairs :]
        total = Collect(part_ref, *refs[:4])
        small = Totals(packed_ref, packed_out, *refs[4:8])
        refs = refs[8:]
        size_of = halving_size()
        sums = [
            take_halving(
                sides[2 * i], sides[2 * i + 1], outs[i], rising[i],
                refs[i * size_of : (i + 1) * size_of],
            )
            for i in range(pairs)
        ]
        greet(True)
        small.start()
        total.start()
        for item in sums:
            item.start()
        interleave(total.relay, range(count - 1, 0, -1), sums + [small], range(bits))
        for step in range(bits, steps):
            small.advance(step)
        total.drain()

        def body(at, size, grad):
            norm_ref[pl.ds(at, size), :] = grad

        total.finish(body)

    shapes = [
        jax.ShapeDtypeStruct((rows, width), jnp.float32),
        jax.ShapeDtypeStruct(packed.shape, jnp.float32),
    ] + [jax.ShapeDtypeStruct((block, home.shape[1]), jnp.float32) for _, home in grads]
    scratch = collect_scratch(part)
    scratch += [pltpu.VMEM((steps,) + packed.shape, jnp.float32)] * 2 + sems(steps)
    for _, home in grads:
        scratch += halving_scratch(home)
    args = (part, packed) + tuple(x for pair in grads for x in pair)
    return call(kernel, 4, shapes, scratch, args)


def on_device(
    tokens_in,
    attn_gain,
    w_query,
    w_key,
    w_value,
    query_gain,
    key_gain,
    w_output,
    mlp_gain,
    w_gate,
    w_up,
    w_down,
    out_cotangent,
):
    f32 = jnp.float32
    head_width = query_gain.shape[0]
    head_count = w_query.shape[1] // head_width
    kv_count = w_key.shape[1] // head_width
    cosine_table, sine_table = rope_tables(SEQ, head_width)
    resid = tokens_in.astype(f32)
    scale_one = row_scale(resid)
    normed_one = spread_rows(tokens_in, attn_gain)
    normed_one, cotangent = lax.optimization_barrier((normed_one, out_cotangent))
    grad_all = gather_rows(cotangent, "tensor")
    tok_count = normed_one.shape[0]
    seq_count = tok_count // SEQ
    query_lin = jnp.dot(normed_one, w_query, preferred_element_type=f32).reshape(
        tok_count, head_count, head_width
    )
    key_lin = jnp.dot(normed_one, w_key, preferred_element_type=f32).reshape(
        tok_count, kv_count, head_width
    )
    value_heads = (
        jnp.dot(normed_one, w_value, preferred_element_type=f32)
        .astype(jnp.bfloat16)
        .reshape(seq_count, SEQ, kv_count, head_width)
    )
    query_scale = row_scale(query_lin)
    key_scale = row_scale(key_lin)
    query_rot = rope_apply(
        (query_lin * query_scale * query_gain).reshape(seq_count, SEQ, head_count, head_width),
        cosine_table,
        sine_table,
    ).astype(jnp.bfloat16)
    key_rot = rope_apply(
        (key_lin * key_scale * key_gain).reshape(seq_count, SEQ, kv_count, head_width),
        cosine_table,
        sine_table,
    ).astype(jnp.bfloat16)
    mixed_heads, log_totals = lax.map(attend_forward, (query_rot, key_rot, value_heads))
    attn_flat = mixed_heads.reshape(tok_count, head_count * head_width)
    attn_part = jnp.dot(attn_flat, w_output, preferred_element_type=f32).astype(jnp.bfloat16)
    attn_part, grad_all = lax.optimization_barrier((attn_part, grad_all))
    hidden, normed_two = finish_attention(attn_part, tokens_in, mlp_gain)
    scale_two = row_scale(hidden)
    gate_lin = jnp.dot(normed_two, w_gate, preferred_element_type=f32)
    up_lin = jnp.dot(normed_two, w_up, preferred_element_type=f32)
    gate_sig = jax.nn.sigmoid(gate_lin)
    activated = (gate_lin * gate_sig * up_lin).astype(jnp.bfloat16)
    grad_act = jnp.dot(grad_all, w_down.T, preferred_element_type=f32)
    grad_gate = (grad_act * up_lin * gate_sig * (1.0 + gate_lin * (1.0 - gate_sig))).astype(
        jnp.bfloat16
    )
    grad_up = (grad_act * gate_lin * gate_sig).astype(jnp.bfloat16)
    back_two = (
        jnp.dot(grad_gate, w_gate.T, preferred_element_type=f32)
        + jnp.dot(grad_up, w_up.T, preferred_element_type=f32)
    ).astype(jnp.bfloat16)
    two_rising = split_columns(normed_two, "dp", True)
    two_falling = split_columns(normed_two, "dp", False)
    first_grads = (
        outer(two_rising, grad_gate),
        outer(two_falling, grad_up),
        outer(split_columns(grad_all, "dp", True), activated),
    )
    grad_hidden, grad_hidden_low, grad_norm_two, grad_w_gate, grad_w_up, grad_down = (
        finish_mlp_back(
            back_two, hidden, out_cotangent, mlp_gain, first_grads, (True, False, True)
        )
    )
    grad_down = grad_down.T
    gain_two = jnp.sum(grad_norm_two * hidden * scale_two, axis=0)
    activated_late, grad_hidden_low = lax.optimization_barrier((activated, grad_hidden_low))
    mlp_part = jnp.dot(activated_late, w_down, preferred_element_type=f32).astype(jnp.bfloat16)
    mlp_sum = scatter_rows(mlp_part, "tensor")
    block_out = (hidden + mlp_sum).astype(jnp.bfloat16)
    output_pair = outer(split_columns(grad_hidden_low, "dp", False), attn_flat)
    grad_mixed = (
        jnp.dot(grad_hidden_low, w_output.T, preferred_element_type=f32)
        .astype(jnp.bfloat16)
        .reshape(seq_count, SEQ, head_count, head_width)
    )
    grad_query_rot, grad_key_rot, grad_values = lax.map(
        attend_backward,
        (query_rot, key_rot, value_heads, mixed_heads, log_totals, grad_mixed),
    )
    grad_query_pre = rope_back(grad_query_rot, cosine_table, sine_table).reshape(
        tok_count, head_count, head_width
    )
    grad_key_pre = rope_back(grad_key_rot, cosine_table, sine_table).reshape(
        tok_count, kv_count, head_width
    )
    gain_query = jnp.sum(grad_query_pre * query_lin * query_scale, axis=(0, 1))
    gain_key = jnp.sum(grad_key_pre * key_lin * key_scale, axis=(0, 1))
    grad_query_low = (
        norm_back(grad_query_pre, query_lin, query_scale, query_gain)
        .astype(jnp.bfloat16)
        .reshape(tok_count, head_count * head_width)
    )
    grad_key_low = (
        norm_back(grad_key_pre, key_lin, key_scale, key_gain)
        .astype(jnp.bfloat16)
        .reshape(tok_count, kv_count * head_width)
    )
    grad_value_low = grad_values.astype(jnp.bfloat16).reshape(tok_count, kv_count * head_width)
    back_full = (
        jnp.dot(grad_query_low, w_query.T, preferred_element_type=f32)
        + jnp.dot(grad_key_low, w_key.T, preferred_element_type=f32)
        + jnp.dot(grad_value_low, w_value.T, preferred_element_type=f32)
    )
    back_one = back_full.astype(jnp.bfloat16)
    gain_one = jnp.sum(back_full * normed_one.astype(f32), axis=0) / attn_gain
    one_rising = split_columns(normed_one, "dp", True)
    one_falling = split_columns(normed_one, "dp", False)
    last_grads = (
        outer(one_rising, grad_query_low),
        output_pair,
        outer(one_falling, grad_key_low),
        outer(one_rising, grad_value_low),
    )
    gains = (gain_one, gain_two, gain_query, gain_key)
    packed = jnp.concatenate(gains)
    lanes = query_gain.shape[0]
    short = -packed.shape[0] % (8 * lanes)
    packed = jnp.pad(packed, (0, short)).reshape(-1, lanes)
    back_one, block_out = lax.optimization_barrier((back_one, block_out))
    grad_norm_one, packed, grad_w_query, grad_w_output, grad_w_key, grad_w_value = finish_all(
        back_one, packed, last_grads, (True, False, False, True)
    )
    grad_w_output = grad_w_output.T
    packed = packed.reshape(-1)
    grad_input = (
        grad_hidden + norm_back(grad_norm_one, resid, scale_one, attn_gain)
    ).astype(jnp.bfloat16)
    ends = []
    at = 0
    for part in gains:
        ends.append(packed[at : at + part.shape[0]])
        at += part.shape[0]
    gain_one, gain_two, gain_query, gain_key = ends
    return (
        block_out,
        grad_input,
        gain_one,
        grad_w_query,
        grad_w_key,
        grad_w_value,
        gain_query,
        gain_key,
        grad_w_output,
        gain_two,
        grad_w_gate,
        grad_w_up,
        grad_down,
    )


def solution(mesh):
    in_specs = (
        P(("dp", "tensor"), None),
        P(),
        P(None, "tensor"),
        P(None, "tensor"),
        P(None, "tensor"),
        P(),
        P(),
        P("tensor", None),
        P(),
        P(None, "tensor"),
        P(None, "tensor"),
        P("tensor", None),
        P(("dp", "tensor"), None),
    )
    out_specs = (
        P(("dp", "tensor"), None),
        P(("dp", "tensor"), None),
        P(),
        P("dp", "tensor"),
        P("dp", "tensor"),
        P("dp", "tensor"),
        P(),
        P(),
        P("tensor", "dp"),
        P(),
        P("dp", "tensor"),
        P("dp", "tensor"),
        P("tensor", "dp"),
    )
    return jax.shard_map(
        on_device, mesh=mesh, in_specs=in_specs, out_specs=out_specs, check_vma=False
    )
```
